32 devices in a mesh: seq: 8 (over z, x), head: 4 (over y, core).
Axes of the slice: x: 2, y: 2, z: 4, core: 2. Of those that a mesh axis runs over, the one named last changes fastest.
Arguments:
- queries: bfloat16 [6144, 2048], P('seq', 'head'), may hold values from -16 to 16
- key_rows: bfloat16 [6144, 2048], P('seq', 'head'), may hold values from -6 to 6
- value_rows: bfloat16 [6144, 2048], P('seq', 'head'), may hold values from -6 to 6
- out_weight: bfloat16 [2048, 3072], P('head'), may hold values from -0.125 to 0.125
- cotangent: bfloat16 [6144, 3072], P('seq', 'head'), may hold values from -6 to 6
- neighbours: int32 [16, 4], P('seq'), may hold values from -1 to 15, as said below
Outputs:
- projected: bfloat16 [6144, 3072], P('seq', 'head')
- grad_queries: bfloat16 [6144, 2048], P('seq', 'head')
- grad_keys: bfloat16 [6144, 2048], P('seq', 'head')
- grad_values: bfloat16 [6144, 2048], P('seq', 'head')
- grad_weight: float32 [2048, 3072], P('head', 'seq')
The draws below stay inside these ranges and needn't reach their ends.
Inputs may be any that keep to these rules, and one draw needn't show every extreme that they name: `neighbours`: slot 0 of tile t holds t; every other slot holds -1 or a tile other than t within 2 tiles of t, no tile twice in a row; the -1 slots of a row come after its tiles.
All inputs are finite; a program needn't handle non-finite values.
Results may differ from the reference program's by a relative error of at most 0.014.
Values may be sent and summed in bfloat16 or wider, within the bound.
A program may use at most 192 MiB of HBM per device.

```python
import math
import jax
import jax.numpy as jnp
from jax import lax

D = 3072
HEADS = 16
HD = 128
TILE = 384
REACH = 2
SLOTS = 4
TOKENS = 6144


def joint_draw(key):
    columns = HEADS * HD
    query_base = jnp.clip(jax.random.normal(jax.random.fold_in(key, 101), (TOKENS, columns), jnp.float32), -6.0, 6.0)
    key_base = jnp.clip(jax.random.normal(jax.random.fold_in(key, 102), (TOKENS, columns), jnp.float32), -6.0, 6.0)
    return (query_base, key_base)


def draw_queries(key, part):
    return joint_draw(key)[0].astype(jnp.bfloat16)


def draw_key_rows(key, part):
    return joint_draw(key)[1].astype(jnp.bfloat16)


def draw_neighbours(key, part):
    tile_total = TOKENS // TILE
    centre = jnp.arange(tile_total, dtype=jnp.int32)[:, None]
    near_offsets = jnp.array([-1, 1], jnp.int32)
    near_target = centre + near_offsets[None, :]
    near_inside = (near_target >= 0) & (near_target < tile_total)
    near = jnp.where(near_inside, near_target, -1)
    far_count = SLOTS - 3
    far_offsets = jnp.concatenate([jnp.arange(-REACH, -1, dtype=jnp.int32), jnp.arange(2, REACH + 1, dtype=jnp.int32)])
    far_total = far_offsets.shape[0]
    rank_keys = jax.random.randint(jax.random.fold_in(key, 201), (tile_total, far_total), 0, 4096) * max(far_total, 1) + jnp.arange(far_total, dtype=jnp.int32)[None, :]
    ordering = jnp.argsort(rank_keys, axis=1)
    far_target = jnp.take_along_axis(centre + far_offsets[None, :], ordering, 1)[:, :far_count]
    far_inside = (far_target >= 0) & (far_target < tile_total)
    kept = jax.random.randint(jax.random.fold_in(key, 202), (tile_total, far_count), 0, 4) != 0
    far = jnp.where(far_inside & kept, far_target, -1)
    others = jnp.concatenate([near, far], axis=1)
    width = SLOTS - 1
    sort_keys = jnp.where(others >= 0, 0, 1) * width + jnp.arange(width, dtype=jnp.int32)[None, :]
    compact = jnp.take_along_axis(others, jnp.argsort(sort_keys, axis=1), 1)
    return jnp.concatenate([centre, compact], axis=1).astype(jnp.int32)


def strengthened(values, own_key, source, target, parts, factor):
    owner, partner = [(jnp.arange(values.shape[axis_at]) // (values.shape[axis_at] // parts)).reshape([-1 if axis == axis_at else 1 for axis in range(values.ndim)]) for axis_at in (source, target)]
    chosen = jax.random.permutation(own_key, parts)[partner]
    strong = (owner == chosen) | (owner == (partner + parts // 2) % parts)
    return jnp.where(strong, factor * values, values)


def block_levels(stream_key, extent, split, least, high):
    factor_of = 1.0
    for position, parts in split:
        steps = jax.random.uniform(jax.random.fold_in(jax.random.fold_in(stream_key, 6), position), (parts,), jnp.float32, least / len(split), high / len(split))
        factor_of = factor_of * jnp.repeat(jnp.exp(steps), extent[position] // parts).reshape((-1,) + (1,) * (len(extent) - 1 - position))
    return factor_of


def centred(key, dims, scale, most, pieces=(), held_as=jnp.bfloat16):
    values = scale * jax.random.normal(key, dims, jnp.float32)
    if pieces:
        values = values * block_levels(key, dims, pieces, -0.22, 0.18)
    return jnp.clip(values, -most, most).astype(held_as)


def gaussian_with(own_key, dims, deviation, reach, shards, heavy, kind=jnp.bfloat16):
    values = deviation * jax.random.normal(own_key, dims, jnp.float32)
    if shards:
        values = values * block_levels(own_key, dims, shards, -0.22, 0.18)
    return jnp.clip(strengthened(values, jax.random.fold_in(own_key, 3), *heavy), -reach, reach).astype(kind)


def setup_inputs(seed: int = 0) -> dict:
    seeds = jax.random.split(jax.random.key(seed), 7)
    queries = draw_queries(jax.random.fold_in(seeds[6], 71), 0)
    key_rows = draw_key_rows(jax.random.fold_in(seeds[6], 71), 0)
    value_rows = centred(seeds[2], (TOKENS, HEADS * HD), 1.0, 6.0, ((0, 8), (1, 4)))
    out_weight = centred(seeds[3], (HEADS * HD, D), (HEADS * HD) ** -0.5, 0.125, ((0, 4),))
    cotangent = gaussian_with(seeds[4], (TOKENS, D), 1.0, 6.0, ((0, 8), (1, 4)), (0, 1, 8, 2.0))
    neighbours = draw_neighbours(jax.random.fold_in(seeds[6], 71), 0)
    return {"queries": queries, "key_rows": key_rows, "value_rows": value_rows, "out_weight": out_weight, "cotangent": cotangent, "neighbours": neighbours}


def reference(queries, key_rows, value_rows, out_weight, cotangent, neighbours):
    columns = HEADS * HD
    score_scale = 1.0 / math.sqrt(HD)
    tile_total = TOKENS // TILE
    grad_attention = jnp.dot(cotangent, out_weight.T, preferred_element_type=jnp.float32).astype(jnp.bfloat16)

    def per_tile(carry, tile_index):
        acc_keys, acc_values = carry
        start_row = (tile_index * TILE).astype(jnp.int32)
        query_tile = lax.dynamic_slice_in_dim(queries, start_row, TILE, 0).astype(jnp.float32).reshape(TILE, HEADS, HD)
        grad_tile = lax.dynamic_slice_in_dim(grad_attention, start_row, TILE, 0).astype(jnp.float32).reshape(TILE, HEADS, HD)
        key_list = []
        value_list = []
        live_list = []
        for slot_index in range(SLOTS):
            neighbour = neighbours[tile_index, slot_index]
            safe_start = (jnp.maximum(neighbour, 0) * TILE).astype(jnp.int32)
            key_list.append(lax.dynamic_slice_in_dim(key_rows, safe_start, TILE, 0))
            value_list.append(lax.dynamic_slice_in_dim(value_rows, safe_start, TILE, 0))
            live_list.append(jnp.broadcast_to(neighbour >= 0, (TILE,)))
        key_block = jnp.concatenate(key_list, 0).astype(jnp.float32).reshape(SLOTS * TILE, HEADS, HD)
        value_block = jnp.concatenate(value_list, 0).astype(jnp.float32).reshape(SLOTS * TILE, HEADS, HD)
        live_keys = jnp.concatenate(live_list, 0)
        scores = jnp.einsum('rhd,khd->hrk', query_tile, key_block) * score_scale
        scores = jnp.where(live_keys[None, None, :], scores, -1e+30)
        row_peak = lax.optimization_barrier(jnp.max(scores, axis=-1, keepdims=True))
        log_total = row_peak + jnp.log(lax.optimization_barrier(jnp.sum(jnp.exp(scores - row_peak), axis=-1, keepdims=True)))
        probabilities = jnp.exp(scores - log_total)
        probs_low = lax.optimization_barrier(probabilities.astype(jnp.bfloat16)).astype(jnp.float32)
        attention_tile = jnp.einsum('hrk,khd->rhd', probs_low, value_block).astype(jnp.bfloat16)
        attention_wide = lax.optimization_barrier(attention_tile).astype(jnp.float32)
        row_delta = lax.optimization_barrier(jnp.sum(grad_tile * attention_wide, axis=-1))
        grad_probs = jnp.einsum('rhd,khd->hrk', grad_tile, value_block)
        grad_scores = probabilities * (grad_probs - jnp.transpose(row_delta)[:, :, None])
        grad_scores = lax.optimization_barrier(grad_scores.astype(jnp.bfloat16)).astype(jnp.float32)
        grad_query = (jnp.einsum('hrk,khd->rhd', grad_scores, key_block) * score_scale).astype(jnp.bfloat16)
        grad_key_block = jnp.einsum('hrk,rhd->khd', grad_scores, query_tile) * score_scale
        grad_value_block = jnp.einsum('hrk,rhd->khd', probs_low, grad_tile)
        for slot_index in range(SLOTS):
            neighbour = neighbours[tile_index, slot_index]
            live_factor = (neighbour >= 0).astype(jnp.float32)
            safe_start = (jnp.maximum(neighbour, 0) * TILE).astype(jnp.int32)
            piece_keys = grad_key_block[slot_index * TILE:(slot_index + 1) * TILE].reshape(TILE, columns) * live_factor
            piece_values = grad_value_block[slot_index * TILE:(slot_index + 1) * TILE].reshape(TILE, columns) * live_factor
            acc_keys = lax.dynamic_update_slice_in_dim(acc_keys, lax.dynamic_slice_in_dim(acc_keys, safe_start, TILE, 0) + piece_keys, safe_start, 0)
            acc_values = lax.dynamic_update_slice_in_dim(acc_values, lax.dynamic_slice_in_dim(acc_values, safe_start, TILE, 0) + piece_values, safe_start, 0)
        return ((acc_keys, acc_values), (attention_tile.reshape(TILE, columns), grad_query.reshape(TILE, columns)))
    empty_acc = jnp.zeros((TOKENS, columns), jnp.float32)
    carried, stacked = lax.scan(per_tile, (empty_acc, empty_acc), jnp.arange(tile_total, dtype=jnp.int32))
    acc_keys, acc_values = carried
    attention_tiles, grad_query_tiles = stacked
    attention = attention_tiles.reshape(TOKENS, columns)
    projected = jnp.dot(attention, out_weight, preferred_element_type=jnp.float32).astype(jnp.bfloat16)
    grad_weight = jnp.dot(attention.T, cotangent, preferred_element_type=jnp.float32) * (1.0 / math.sqrt(TOKENS))
    return (projected, grad_query_tiles.reshape(TOKENS, columns), acc_keys.astype(jnp.bfloat16), acc_values.astype(jnp.bfloat16), grad_weight)
```

```python
import functools
import math

import jax
import jax.numpy as jnp
from jax import lax
from jax.experimental import pallas as pl
from jax.experimental.pallas import tpu as pltpu
from jax.sharding import PartitionSpec as P

HD = 128
TILE = 384
REACH = 2
SLOTS = 4
RIM = REACH * TILE
F32 = jnp.float32
BF16 = jnp.bfloat16


def dot_nt(a, b):
    return lax.dot_general(a, b, (((1,), (1,)), ((), ())), preferred_element_type=F32)


def dot_nn(a, b):
    return lax.dot_general(a, b, (((1,), (0,)), ((), ())), preferred_element_type=F32)


def dot_tn(a, b):
    return lax.dot_general(a, b, (((0,), (0,)), ((), ())), preferred_element_type=F32)


def fold(op, x):
    out = x[:, :HD]
    for i in range(1, x.shape[1] // HD):
        out = op(out, x[:, i * HD : (i + 1) * HD])
    return out


def attend(rows, tiles, place, count, q, g, km, vm, far, near, att, dq, mid, rim_far, rim_near, kx, vx, dk, dv, scr):
    t = pl.program_id(1)
    scale = 1.0 / math.sqrt(HD)
    c = scale * math.log2(math.e)
    hi = RIM + rows

    @pl.when(t == 0)
    def _():
        kx[:RIM] = far[0]
        kx[RIM:hi] = km[...]
        kx[hi:] = near[0]
        vx[:RIM] = far[1]
        vx[RIM:hi] = vm[...]
        vx[hi:] = near[1]
        dk[...] = jnp.zeros_like(dk)
        dv[...] = jnp.zeros_like(dv)

    live = count[t]
    qv = q[...]
    gv = g[...]

    def at(j):
        return pl.ds(pl.multiple_of(place[t * SLOTS + j] * TILE, TILE), TILE)

    def score(j, m):
        s = dot_nt(qv, kx[at(j), :])
        scr[j] = s
        return jnp.maximum(m, fold(jnp.maximum, s))

    m = lax.fori_loop(0, live, score, jnp.full((TILE, HD), -3e38, F32))
    m = jnp.max(m, axis=1, keepdims=True)

    def soft(j, carry):
        total, acc = carry
        e = jnp.exp2((scr[j] - m) * c)
        scr[j] = e
        return total + fold(jnp.add, e), acc + dot_nn(e.astype(BF16), vx[at(j), :])

    zero = jnp.zeros((TILE, HD), F32)
    total, acc = lax.fori_loop(0, live, soft, (zero, zero))
    inv = 1.0 / jnp.sum(total, axis=1, keepdims=True)
    out = (acc * inv).astype(BF16)
    att[...] = out
    delta = jnp.sum(gv.astype(F32) * out.astype(F32), axis=1, keepdims=True)

    def back(j, acc):
        here = at(j)
        k = kx[here, :]
        p = scr[j] * inv
        ds = (p * (dot_nt(gv, vx[here, :]) - delta)).astype(BF16)
        dv[here, :] += dot_tn(p.astype(BF16), gv)
        dk[here, :] += dot_tn(ds, qv)
        return acc + dot_nn(ds, k)

    dq[...] = (lax.fori_loop(0, live, back, zero) * scale).astype(BF16)

    @pl.when(t == tiles - 1)
    def _():
        rim_far[0] = (dk[:RIM] * scale).astype(BF16)
        rim_far[1] = dv[:RIM].astype(BF16)
        mid[0] = dk[RIM:hi] * scale
        mid[1] = dv[RIM:hi]
        rim_near[0] = dk[hi:] * scale
        rim_near[1] = dv[hi:]


def attention_call(place, count, q, g, k, v, far, near, first, heads):
    rows = q.shape[0]
    tiles = rows // TILE
    ext = rows + 2 * RIM
    cols = heads * HD
    tile_in = pl.BlockSpec((TILE, HD), lambda h, t, *_: (t, first + h))
    slab_in = pl.BlockSpec((rows, HD), lambda h, t, *_: (0, first + h))
    rim = pl.BlockSpec((2, RIM, HD), lambda h, t, *_: (0, 0, h))
    tile_out = pl.BlockSpec((TILE, HD), lambda h, t, *_: (t, h))
    mid = pl.BlockSpec((2, rows, HD), lambda h, t, *_: (0, 0, h))
    pairs = heads * tiles * SLOTS
    return pl.pallas_call(
        functools.partial(attend, rows, tiles),
        grid_spec=pltpu.PrefetchScalarGridSpec(
            num_scalar_prefetch=2,
            grid=(heads, tiles),
            in_specs=[tile_in, tile_in, slab_in, slab_in, rim, rim],
            out_specs=[tile_out, tile_out, mid, rim, rim],
            scratch_shapes=[
                pltpu.VMEM((ext, HD), BF16),
                pltpu.VMEM((ext, HD), BF16),
                pltpu.VMEM((ext, HD), F32),
                pltpu.VMEM((ext, HD), F32),
                pltpu.VMEM((SLOTS, TILE, TILE), F32),
            ],
        ),
        out_shape=[
            jax.ShapeDtypeStruct((rows, cols), BF16),
            jax.ShapeDtypeStruct((rows, cols), BF16),
            jax.ShapeDtypeStruct((2, rows, cols), F32),
            jax.ShapeDtypeStruct((2, RIM, cols), BF16),
            jax.ShapeDtypeStruct((2, RIM, cols), F32),
        ],
        compiler_params=pltpu.CompilerParams(
            dimension_semantics=("arbitrary", "arbitrary"), vmem_limit_bytes=40 << 20
        ),
        cost_estimate=pl.CostEstimate(
            flops=pairs * 12 * TILE * TILE * HD,
            bytes_accessed=rows * cols * 40,
            transcendentals=pairs * TILE * TILE,
        ),
    )(place, count, q, g, k, v, far, near)


def swap(x, axis, bit):
    return lax.ppermute(x, axis, [(i, i ^ bit) for i in range(lax.axis_size(axis))])


def shift(x, axis, even_step):
    size = lax.axis_size(axis)
    pairs = [(i, i + (even_step if i % 2 == 0 else -even_step)) for i in range(size)]
    return lax.ppermute(x, axis, [(i, j) for i, j in pairs if 0 <= j < size])


def local(queries, key_rows, value_rows, out_weight, cotangent, neighbours):
    rows, columns = queries.shape
    heads = columns // HD
    tiles = rows // TILE
    seq, head = lax.axis_size("seq"), lax.axis_size("head")
    s, h = lax.axis_index("seq"), lax.axis_index("head")
    paired = head == 4 and seq == 8
    width = cotangent.shape[1]
    piece = width * head // seq
    norm = 1.0 / math.sqrt(rows * seq)
    chunks = 2
    per = heads // chunks

    halos = []
    for n in range(chunks):
        cut = slice(n * per * HD, (n + 1) * per * HD)
        kv = jnp.stack([key_rows[:, cut], value_rows[:, cut]])
        near = swap(kv, "seq", 1)
        far = shift(near, "seq", 2)
        halos.append((far, near))

    if paired:
        shards = [cotangent, swap(cotangent, "head", 1), swap(cotangent, "head", 2)]
        shards.append(swap(shards[2], "head", 1))
        weights = [
            lax.dynamic_slice_in_dim(out_weight, (h ^ r) * width, width, 1) for r in range(4)
        ]
        grad_attention = sum(dot_nt(a, b) for a, b in zip(shards, weights)).astype(BF16)
    else:
        full = lax.all_gather(cotangent, "head", axis=1, tiled=True)
        grad_attention = dot_nt(full, out_weight).astype(BF16)

    first = s * tiles - REACH
    alive = neighbours >= 0
    index = jnp.where(alive, neighbours - first, 0)
    span = tiles + REACH
    odd = s % 2 == 1
    turned = jnp.where(index < REACH, index + span, jnp.where(index >= span, index - span, index))
    place = jnp.where(odd, turned, index).reshape(-1).astype(jnp.int32)
    count = jnp.sum(alive, axis=1).astype(jnp.int32)

    atts, dqs, dks, dvs, gws = [], [], [], [], []
    for n in range(chunks):
        far, near = halos[n]
        att, dq, mid, rim_far, rim_near = attention_call(
            place, count, queries, grad_attention, key_rows, value_rows, far, near, n * per, per
        )
        relayed = shift(rim_far, "seq", -2)
        back = swap((rim_near + relayed.astype(F32)).astype(BF16), "seq", 1)
        done = (mid + back.astype(F32)).astype(BF16)
        atts.append(att)
        dqs.append(dq)
        dks.append(done[0])
        dvs.append(done[1])

    attention = jnp.concatenate(atts, axis=1)
    if paired:
        parts = [dot_nn(attention, w) for w in weights]
        sent = jnp.stack([parts[1], parts[3]]).astype(BF16)
        got = swap(sent, "head", 1).astype(F32)
        other = swap((parts[2] + got[1]).astype(BF16), "head", 2)
        projected = (parts[0] + got[0] + other.astype(F32)).astype(BF16)
        stacked = jnp.stack(shards)
        z, x = s // 2, s % 2
        turn = h ^ z

        def columns_of(k, side):
            block = lax.dynamic_index_in_dim(stacked, turn ^ k, 0, False)
            return lax.dynamic_slice_in_dim(block, side * piece, piece, 1)

        send = jnp.stack([columns_of(k, 1 - x) for k in range(4)])
        keep = jnp.stack([columns_of(k, x) for k in range(4)])
        away = jnp.einsum("tc,ktd->kcd", attention, send, preferred_element_type=F32)
        stay = jnp.einsum("tc,ktd->kcd", attention, keep, preferred_element_type=F32)
        stay = stay + swap(away.astype(BF16), "seq", 1).astype(F32)
        got = swap(jnp.stack([stay[1], stay[3]]).astype(BF16), "seq", 2).astype(F32)
        last = swap((stay[2] + got[1]).astype(BF16), "seq", 4).astype(F32)
        grad_weight = (stay[0] + got[0] + last) * norm
    else:
        projected = lax.psum_scatter(
            dot_nn(attention, out_weight).astype(BF16), "head", scatter_dimension=1, tiled=True
        )
        grad_weight = (
            lax.psum_scatter(
                dot_tn(attention, full).astype(BF16), "seq", scatter_dimension=1, tiled=True
            ).astype(F32)
            * norm
        )
    return (
        projected,
        jnp.concatenate(dqs, axis=1),
        jnp.concatenate(dks, axis=1),
        jnp.concatenate(dvs, axis=1),
        grad_weight,
    )


def solution(mesh):
    both = P("seq", "head")
    return jax.shard_map(
        local,
        mesh=mesh,
        in_specs=(both, both, both, P("head", None), both, P("seq", None)),
        out_specs=(both, both, both, both, P("head", "seq")),
        check_vma=False,
    )
```

```python
import functools
import math

import jax
import jax.numpy as jnp
from jax import lax
from jax.experimental import pallas as pl
from jax.experimental.pallas import tpu as pltpu
from jax.sharding import PartitionSpec as P

HD = 128
TILE = 384
REACH = 2
SLOTS = 4
RIM = REACH * TILE
F32 = jnp.float32
BF16 = jnp.bfloat16


def dot_nt(a, b):
    return lax.dot_general(a, b, (((1,), (1,)), ((), ())), preferred_element_type=F32)


def dot_nn(a, b):
    return lax.dot_general(a, b, (((1,), (0,)), ((), ())), preferred_element_type=F32)


def dot_tn(a, b):
    return lax.dot_general(a, b, (((0,), (0,)), ((), ())), preferred_element_type=F32)


def fold(op, x):
    out = x[:, :HD]
    for i in range(1, x.shape[1] // HD):
        out = op(out, x[:, i * HD : (i + 1) * HD])
    return out


def attend(rows, tiles, place, count, q, g, km, vm, far, near, att, dq, mid, rim_far, rim_near, kx, vx, dk, dv, scr):
    t = pl.program_id(1)
    scale = 1.0 / math.sqrt(HD)
    c = scale * math.log2(math.e)
    hi = RIM + rows

    @pl.when(t == 0)
    def _():
        kx[:RIM] = far[0]
        kx[RIM:hi] = km[...]
        kx[hi:] = near[0]
        vx[:RIM] = far[1]
        vx[RIM:hi] = vm[...]
        vx[hi:] = near[1]
        dk[...] = jnp.zeros_like(dk)
        dv[...] = jnp.zeros_like(dv)

    live = count[t]
    qv = q[...]
    gv = g[...]

    def at(j):
        return pl.ds(pl.multiple_of(place[t * SLOTS + j] * TILE, TILE), TILE)

    def score(j, m):
        s = dot_nt(qv, kx[at(j), :])
        scr[j] = s
        return jnp.maximum(m, fold(jnp.maximum, s))

    m = lax.fori_loop(0, live, score, jnp.full((TILE, HD), -3e38, F32))
    m = jnp.max(m, axis=1, keepdims=True)

    def soft(j, carry):
        total, acc = carry
        e = jnp.exp2((scr[j] - m) * c)
        scr[j] = e
        return total + fold(jnp.add, e), acc + dot_nn(e.astype(BF16), vx[at(j), :])

    zero = jnp.zeros((TILE, HD), F32)
    total, acc = lax.fori_loop(0, live, soft, (zero, zero))
    inv = 1.0 / jnp.sum(total, axis=1, keepdims=True)
    out = (acc * inv).astype(BF16)
    att[...] = out
    delta = jnp.sum(gv.astype(F32) * out.astype(F32), axis=1, keepdims=True)

    def back(j, acc):
        here = at(j)
        k = kx[here, :]
        p = scr[j] * inv
        ds = (p * (dot_nt(gv, vx[here, :]) - delta)).astype(BF16)
        dv[here, :] += dot_tn(p.astype(BF16), gv)
        dk[here, :] += dot_tn(ds, qv)
        return acc + dot_nn(ds, k)

    dq[...] = (lax.fori_loop(0, live, back, zero) * scale).astype(BF16)

    @pl.when(t == tiles - 1)
    def _():
        rim_far[0] = (dk[:RIM] * scale).astype(BF16)
        rim_far[1] = dv[:RIM].astype(BF16)
        mid[0] = dk[RIM:hi] * scale
        mid[1] = dv[RIM:hi]
        rim_near[0] = dk[hi:] * scale
        rim_near[1] = dv[hi:]


def attention_call(place, count, q, g, k, v, far, near, first, offset, heads):
    rows = q.shape[0]
    tiles = rows // TILE
    ext = rows + 2 * RIM
    cols = heads * HD
    tile_in = pl.BlockSpec((TILE, HD), lambda h, t, *_: (t, first + h))
    slab_in = pl.BlockSpec((rows, HD), lambda h, t, *_: (0, first + h))
    rim_in = pl.BlockSpec((2, RIM, HD), lambda h, t, *_: (0, 0, offset + h))
    rim = pl.BlockSpec((2, RIM, HD), lambda h, t, *_: (0, 0, h))
    tile_out = pl.BlockSpec((TILE, HD), lambda h, t, *_: (t, h))
    mid = pl.BlockSpec((2, rows, HD), lambda h, t, *_: (0, 0, h))
    pairs = heads * tiles * SLOTS
    return pl.pallas_call(
        functools.partial(attend, rows, tiles),
        grid_spec=pltpu.PrefetchScalarGridSpec(
            num_scalar_prefetch=2,
            grid=(heads, tiles),
            in_specs=[tile_in, tile_in, slab_in, slab_in, rim_in, rim_in],
            out_specs=[tile_out, tile_out, mid, rim, rim],
            scratch_shapes=[
                pltpu.VMEM((ext, HD), BF16),
                pltpu.VMEM((ext, HD), BF16),
                pltpu.VMEM((ext, HD), F32),
                pltpu.VMEM((ext, HD), F32),
                pltpu.VMEM((SLOTS, TILE, TILE), F32),
            ],
        ),
        out_shape=[
            jax.ShapeDtypeStruct((rows, cols), BF16),
            jax.ShapeDtypeStruct((rows, cols), BF16),
            jax.ShapeDtypeStruct((2, rows, cols), F32),
            jax.ShapeDtypeStruct((2, RIM, cols), BF16),
            jax.ShapeDtypeStruct((2, RIM, cols), F32),
        ],
        compiler_params=pltpu.CompilerParams(
            dimension_semantics=("arbitrary", "arbitrary"), vmem_limit_bytes=40 << 20
        ),
        cost_estimate=pl.CostEstimate(
            flops=pairs * 12 * TILE * TILE * HD,
            bytes_accessed=rows * cols * 40,
            transcendentals=pairs * TILE * TILE,
        ),
    )(place, count, q, g, k, v, far, near)


def weight_terms(turned, side, one, two, away_cols, stay_cols, away, stay):
    a = jnp.concatenate([one[...], two[...]], axis=1)
    away[0] = dot_tn(a, away_cols[0]).astype(BF16)
    stay[0] = dot_tn(a, stay_cols[0])


def weight_call(turned, side, one, two, stacked, piece):
    rows = one.shape[0]
    whole = pl.BlockSpec((rows, HD), lambda k, *_: (0, 0))
    out = pl.BlockSpec((1, 2 * HD, piece), lambda k, *_: (k, 0, 0))
    return pl.pallas_call(
        weight_terms,
        grid_spec=pltpu.PrefetchScalarGridSpec(
            num_scalar_prefetch=2,
            grid=(4,),
            in_specs=[
                whole,
                whole,
                pl.BlockSpec((1, rows, piece), lambda k, t, x: (t[k], 0, 1 - x[0])),
                pl.BlockSpec((1, rows, piece), lambda k, t, x: (t[k], 0, x[0])),
            ],
            out_specs=[out, out],
        ),
        out_shape=[
            jax.ShapeDtypeStruct((4, 2 * HD, piece), BF16),
            jax.ShapeDtypeStruct((4, 2 * HD, piece), F32),
        ],
        compiler_params=pltpu.CompilerParams(dimension_semantics=("arbitrary",), vmem_limit_bytes=40 << 20),
        cost_estimate=pl.CostEstimate(
            flops=2 * rows * 2 * HD * piece * 8, bytes_accessed=rows * piece * 24, transcendentals=0
        ),
    )(turned, side, one, two, stacked, stacked)


def swap(x, axis, bit):
    return lax.ppermute(x, axis, [(i, i ^ bit) for i in range(lax.axis_size(axis))])


def shift(x, axis, even_step):
    size = lax.axis_size(axis)
    pairs = [(i, i + (even_step if i % 2 == 0 else -even_step)) for i in range(size)]
    return lax.ppermute(x, axis, [(i, j) for i, j in pairs if 0 <= j < size])


def local(queries, key_rows, value_rows, out_weight, cotangent, neighbours):
    rows, columns = queries.shape
    heads = columns // HD
    tiles = rows // TILE
    seq, head = lax.axis_size("seq"), lax.axis_size("head")
    s, h = lax.axis_index("seq"), lax.axis_index("head")
    paired = head == 4 and seq == 8
    width = cotangent.shape[1]
    piece = width * head // seq
    norm = 1.0 / math.sqrt(rows * seq)
    chunks = 2
    per = heads // chunks

    halos = []
    packs = []
    for n in range(chunks):
        cut = slice(n * per * HD, (n + 1) * per * HD)
        packs.append(jnp.stack([key_rows[:, cut], value_rows[:, cut]]))
    for n in range(chunks):
        near = swap(packs[n], "seq", 1)
        far = shift(near, "seq", 2)
        halos.append((far, near))

    if paired:
        cot, _ = lax.optimization_barrier((cotangent, packs[0]))
        shards = [cot, swap(cot, "head", 1), swap(cot, "head", 2)]
        shards.append(swap(shards[2], "head", 1))
        weights = [
            lax.dynamic_slice_in_dim(out_weight, (h ^ r) * width, width, 1) for r in range(4)
        ]
        grad_attention = sum(dot_nt(a, b) for a, b in zip(shards, weights)).astype(BF16)
        stacked = jnp.stack(shards)
        turned = ((h ^ (s // 2)) ^ jnp.arange(4, dtype=jnp.int32)).astype(jnp.int32)
        side = (s % 2).astype(jnp.int32).reshape(1)
    else:
        full = lax.all_gather(cotangent, "head", axis=1, tiled=True)
        grad_attention = dot_nt(full, out_weight).astype(BF16)

    first = s * tiles - REACH
    alive = neighbours >= 0
    index = jnp.where(alive, neighbours - first, 0)
    span = tiles + REACH
    odd = s % 2 == 1
    far_first = jnp.where(
        index < REACH, index + span, jnp.where(index >= span, index - span, index)
    )
    place = jnp.where(odd, far_first, index).reshape(-1).astype(jnp.int32)
    count = jnp.sum(alive, axis=1).astype(jnp.int32)

    atts, dqs, mids, nears, relays, terms = [], [], [], [], [], []
    for n in range(heads):
        far, near = halos[n // per]
        if n >= 2:
            place, relays[n - 2] = lax.optimization_barrier((place, relays[n - 2]))
        if n == 3 and terms:
            place, away = lax.optimization_barrier((place, terms[0][0]))
            terms[0] = (away, terms[0][1])
        att, dq, mid, rim_far, rim_near = attention_call(
            place, count, queries, grad_attention, key_rows, value_rows, far, near, n, n % per, 1
        )
        relays.append(shift(rim_far, "seq", -2))
        atts.append(att)
        dqs.append(dq)
        mids.append(mid)
        nears.append(rim_near)
        if paired and n % 2 == 1:
            terms.append(weight_call(turned, side, atts[n - 1], att, stacked, piece))

    dks, dvs = [], []
    for n in range(heads):
        back = swap((nears[n] + relays[n].astype(F32)).astype(BF16), "seq", 1)
        done = (mids[n] + back.astype(F32)).astype(BF16)
        dks.append(done[0])
        dvs.append(done[1])

    attention = jnp.concatenate(atts, axis=1)
    if paired:
        parts = [dot_nn(attention, w) for w in weights]
        sent = jnp.stack([parts[1], parts[3]]).astype(BF16)
        got = swap(sent, "head", 1).astype(F32)
        other = swap((parts[2] + got[1]).astype(BF16), "head", 2)
        projected = (parts[0] + got[0] + other.astype(F32)).astype(BF16)
        pieces = []
        for away, stay in terms:
            stay = stay + swap(away, "seq", 1).astype(F32)
            got = swap(jnp.stack([stay[1], stay[3]]).astype(BF16), "seq", 2).astype(F32)
            last = swap((stay[2] + got[1]).astype(BF16), "seq", 4).astype(F32)
            pieces.append((stay[0] + got[0] + last) * norm)
        grad_weight = jnp.concatenate(pieces, axis=0)
    else:
        projected = lax.psum_scatter(
            dot_nn(attention, out_weight).astype(BF16), "head", scatter_dimension=1, tiled=True
        )
        grad_weight = (
            lax.psum_scatter(
                dot_tn(attention, full).astype(BF16), "seq", scatter_dimension=1, tiled=True
            ).astype(F32)
            * norm
        )
    return (
        projected,
        jnp.concatenate(dqs, axis=1),
        jnp.concatenate(dks, axis=1),
        jnp.concatenate(dvs, axis=1),
        grad_weight,
    )


def solution(mesh):
    both = P("seq", "head")
    return jax.shard_map(
        local,
        mesh=mesh,
        in_specs=(both, both, both, P("head", None), both, P("seq", None)),
        out_specs=(both, both, both, both, P("head", "seq")),
        check_vma=False,
    )
```

```python
import functools
import math

import jax
import jax.numpy as jnp
from jax import lax
from jax.experimental import pallas as pl
from jax.experimental.pallas import tpu as pltpu
from jax.sharding import PartitionSpec as P

HD = 128
TILE = 384
REACH = 2
SLOTS = 4
RIM = REACH * TILE
F32 = jnp.float32
BF16 = jnp.bfloat16


def dot_nt(a, b):
    return lax.dot_general(a, b, (((1,), (1,)), ((), ())), preferred_element_type=F32)


def dot_nn(a, b):
    return lax.dot_general(a, b, (((1,), (0,)), ((), ())), preferred_element_type=F32)


def dot_tn(a, b):
    return lax.dot_general(a, b, (((0,), (0,)), ((), ())), preferred_element_type=F32)


def fold(op, x):
    out = x[:, :HD]
    for i in range(1, x.shape[1] // HD):
        out = op(out, x[:, i * HD : (i + 1) * HD])
    return out


def attend(rows, tiles, place, count, q, g, km, vm, far, near, att, dq, mid, rim_far, rim_near, kx, vx, dk, dv, scr):
    t = pl.program_id(1)
    scale = 1.0 / math.sqrt(HD)
    c = scale * math.log2(math.e)
    hi = RIM + rows

    @pl.when(t == 0)
    def _():
        kx[:RIM] = far[0]
        kx[RIM:hi] = km[...]
        kx[hi:] = near[0]
        vx[:RIM] = far[1]
        vx[RIM:hi] = vm[...]
        vx[hi:] = near[1]
        dk[...] = jnp.zeros_like(dk)
        dv[...] = jnp.zeros_like(dv)

    live = count[t]
    qv = q[...]
    gv = g[...]

    def at(j):
        return pl.ds(pl.multiple_of(place[t * SLOTS + j] * TILE, TILE), TILE)

    def score(j, m):
        s = dot_nt(qv, kx[at(j), :])
        scr[j] = s
        return jnp.maximum(m, fold(jnp.maximum, s))

    m = lax.fori_loop(0, live, score, jnp.full((TILE, HD), -3e38, F32))
    m = jnp.max(m, axis=1, keepdims=True)

    def soft(j, carry):
        total, acc = carry
        e = jnp.exp2((scr[j] - m) * c)
        scr[j] = e
        return total + fold(jnp.add, e), acc + dot_nn(e.astype(BF16), vx[at(j), :])

    zero = jnp.zeros((TILE, HD), F32)
    total, acc = lax.fori_loop(0, live, soft, (zero, zero))
    inv = 1.0 / jnp.sum(total, axis=1, keepdims=True)
    out = (acc * inv).astype(BF16)
    att[...] = out
    delta = jnp.sum(gv.astype(F32) * out.astype(F32), axis=1, keepdims=True)

    def back(j, acc):
        here = at(j)
        k = kx[here, :]
        p = scr[j] * inv
        ds = (p * (dot_nt(gv, vx[here, :]) - delta)).astype(BF16)
        dv[here, :] += dot_tn(p.astype(BF16), gv)
        dk[here, :] += dot_tn(ds, qv)
        return acc + dot_nn(ds, k)

    dq[...] = (lax.fori_loop(0, live, back, zero) * scale).astype(BF16)

    @pl.when(t == tiles - 1)
    def _():
        rim_far[0] = (dk[:RIM] * scale).astype(BF16)
        rim_far[1] = dv[:RIM].astype(BF16)
        mid[0] = dk[RIM:hi] * scale
        mid[1] = dv[RIM:hi]
        rim_near[0] = dk[hi:] * scale
        rim_near[1] = dv[hi:]


def attention_call(place, count, q, g, k, v, far, near, first, heads):
    rows = q.shape[0]
    tiles = rows // TILE
    ext = rows + 2 * RIM
    cols = heads * HD
    tile_in = pl.BlockSpec((TILE, HD), lambda h, t, *_: (t, first + h))
    slab_in = pl.BlockSpec((rows, HD), lambda h, t, *_: (0, first + h))
    rim = pl.BlockSpec((2, RIM, HD), lambda h, t, *_: (0, 0, h))
    tile_out = pl.BlockSpec((TILE, HD), lambda h, t, *_: (t, h))
    mid = pl.BlockSpec((2, rows, HD), lambda h, t, *_: (0, 0, h))
    pairs = heads * tiles * SLOTS
    return pl.pallas_call(
        functools.partial(attend, rows, tiles),
        grid_spec=pltpu.PrefetchScalarGridSpec(
            num_scalar_prefetch=2,
            grid=(heads, tiles),
            in_specs=[tile_in, tile_in, slab_in, slab_in, rim, rim],
            out_specs=[tile_out, tile_out, mid, rim, rim],
            scratch_shapes=[
                pltpu.VMEM((ext, HD), BF16),
                pltpu.VMEM((ext, HD), BF16),
                pltpu.VMEM((ext, HD), F32),
                pltpu.VMEM((ext, HD), F32),
                pltpu.VMEM((SLOTS, TILE, TILE), F32),
            ],
        ),
        out_shape=[
            jax.ShapeDtypeStruct((rows, cols), BF16),
            jax.ShapeDtypeStruct((rows, cols), BF16),
            jax.ShapeDtypeStruct((2, rows, cols), F32),
            jax.ShapeDtypeStruct((2, RIM, cols), BF16),
            jax.ShapeDtypeStruct((2, RIM, cols), F32),
        ],
        compiler_params=pltpu.CompilerParams(
            dimension_semantics=("arbitrary", "arbitrary"), vmem_limit_bytes=40 << 20
        ),
        cost_estimate=pl.CostEstimate(
            flops=pairs * 12 * TILE * TILE * HD,
            bytes_accessed=rows * cols * 40,
            transcendentals=pairs * TILE * TILE,
        ),
    )(place, count, q, g, k, v, far, near)


def swap(x, axis, bit):
    return lax.ppermute(x, axis, [(i, i ^ bit) for i in range(lax.axis_size(axis))])


def shift(x, axis, even_step):
    size = lax.axis_size(axis)
    pairs = [(i, i + (even_step if i % 2 == 0 else -even_step)) for i in range(size)]
    return lax.ppermute(x, axis, [(i, j) for i, j in pairs if 0 <= j < size])


MESH = pl.DeviceIdType.MESH


def finish(
    chunks, seq, norm,
    att, stacked, weight, rim_far, rim_near, mid,
    projected, dkv, grad_weight,
    far_in, near_out, near_in, gw_out, gw_in, gw_sum, two_out, two_in, four_out, four_in,
    core_out, core_in, mine, theirs, y_out, y_in,
    far_s, far_r, near_s, near_r, gw_s, gw_r, two_s, two_r, four_s, four_r, core_s, core_r, y_s, y_r,
):
    s, h = lax.axis_index("seq"), lax.axis_index("head")
    x, z0, z1 = s % 2, (s // 2) % 2, (s // 4) % 2
    h0, h1 = h % 2, (h // 2) % 2
    beside = (s + 1 - 2 * x, h)
    hop2 = (s + 2 - 4 * z0, h)
    hop4 = (s + 4 - 8 * z1, h)
    mate = (s, h + 1 - 2 * h0)
    across = (s, h + 2 - 4 * h1)
    below, above = s >= 2, s + 2 < seq
    width = projected.shape[1]
    piece = grad_weight.shape[1]
    part = att[0].shape[1]

    def send(src, dst, sems, semr, i, dev):
        return pltpu.make_async_remote_copy(
            src_ref=src, dst_ref=dst, send_sem=sems.at[i], recv_sem=semr.at[i],
            device_id=dev, device_id_type=MESH,
        )

    barrier = pltpu.get_barrier_semaphore()
    for dev in (beside, hop4, mate, across):
        pl.semaphore_signal(barrier, inc=1, device_id=dev, device_id_type=MESH)

    @pl.when(below)
    def _():
        pl.semaphore_signal(barrier, inc=1, device_id=(s - 2, h), device_id_type=MESH)

    @pl.when(above)
    def _():
        pl.semaphore_signal(barrier, inc=1, device_id=(s + 2, h), device_id_type=MESH)

    pl.semaphore_wait(barrier, 4 + (s + seq - 2) // seq + (2 * seq - 3 - s) // seq)

    down = s - 2 + 4 * x
    sends_far = (down >= 0) & (down < seq)
    up = s + 2 - 4 * x
    gets_far = (up >= 0) & (up < seq)
    fars = [send(rim_far[c], far_in.at[c], far_s, far_r, c, (down, h)) for c in range(chunks)]

    @pl.when(sends_far)
    def _():
        for copy in fars:
            copy.start()

    def columns(k, side):
        r = (h0 + z0 + k % 2) % 2 + 2 * ((h1 + z1 + k // 2) % 2)
        return stacked[r, :, pl.ds(pl.multiple_of(side * piece, piece), piece)]

    gws = []
    for k in (1, 3, 2, 0):
        cot = columns(k, 1 - x)
        for c in range(chunks):
            gw_out[k, c * part : (c + 1) * part] = dot_tn(att[c][...], cot).astype(BF16)
        gws.append(send(gw_out.at[k], gw_in.at[k], gw_s, gw_r, k, beside))
        gws[-1].start()

    def share(r):
        b0, b1 = (h0 + r % 2) % 2, (h1 + r // 2) % 2
        at = pl.ds(pl.multiple_of((b0 + 2 * b1) * width, width), width)
        total = dot_nn(att[0][...], weight[:part, at])
        for c in range(1, chunks):
            total += dot_nn(att[c][...], weight[c * part : (c + 1) * part, at])
        return total

    cores = []
    for i, r in enumerate((3, 1)):
        core_out[i] = share(r).astype(BF16)
        cores.append(send(core_out.at[i], core_in.at[i], core_s, core_r, i, mate))
        cores[-1].start()
    theirs[...] = share(2)
    cores[0].wait_recv()
    y_out[...] = (theirs[...] + core_in[0].astype(F32)).astype(BF16)
    ys = send(y_out, y_in, y_s, y_r, 0, across)
    ys.start()

    nears = []
    for c in range(chunks):
        nears.append(send(near_out.at[c], near_in.at[c], near_s, near_r, c, beside))

        @pl.when(gets_far)
        def _():
            fars[c].wait_recv()
            for i in range(2):
                near_out[c, i] = (rim_near[c][i] + far_in[c, i].astype(F32)).astype(BF16)

        @pl.when(jnp.logical_not(gets_far))
        def _():
            for i in range(2):
                near_out[c, i] = rim_near[c][i].astype(BF16)

        nears[c].start()

    for k in range(4):
        cot = columns(k, x)
        for c in range(chunks):
            gw_sum[k, c * part : (c + 1) * part] = dot_tn(att[c][...], cot)
    mine[...] = share(0)
    cores[1].wait_recv()
    mine[...] += core_in[1].astype(F32)

    twos = []
    for i, k in enumerate((1, 3)):
        gws[i].wait_recv()
        two_out[i] = (gw_sum[k] + gw_in[k].astype(F32)).astype(BF16)
        twos.append(send(two_out.at[i], two_in.at[i], two_s, two_r, i, hop2))
    twos[1].start()
    twos[0].start()
    gws[2].wait_recv()
    gw_sum[2] += gw_in[2].astype(F32)
    gws[3].wait_recv()
    gw_sum[0] += gw_in[0].astype(F32)
    twos[1].wait_recv()
    four_out[...] = (gw_sum[2] + two_in[1].astype(F32)).astype(BF16)
    four = send(four_out, four_in, four_s, four_r, 0, hop4)
    four.start()
    twos[0].wait_recv()
    gw_sum[0] += two_in[0].astype(F32)

    ys.wait_recv()
    projected[...] = (mine[...] + y_in[...].astype(F32)).astype(BF16)
    four.wait_recv()
    grad_weight[...] = (gw_sum[0] + four_in[...].astype(F32)) * norm
    for c in range(chunks):
        nears[c].wait_recv()
        for i in range(2):
            dkv[i, :, c * part : (c + 1) * part] = (mid[c][i] + near_in[c, i].astype(F32)).astype(BF16)

    @pl.when(sends_far)
    def _():
        for copy in fars:
            copy.wait_send()

    for copy in gws + cores + nears + twos + [ys, four]:
        copy.wait_send()


def finish_call(atts, stacked, weight, fars, nears, mids, seq, norm):
    chunks = len(atts)
    rows, part = atts[0].shape
    depth = chunks * part
    width = stacked.shape[2]
    piece = width * 4 // seq
    vmem = pl.BlockSpec(memory_space=pltpu.VMEM)
    rim = (chunks, 2, RIM, part)
    sem = pltpu.SemaphoreType.DMA

    def kernel(*refs):
        refs = list(refs)

        def take(n):
            got = refs[:n]
            del refs[:n]
            return got

        att = take(chunks)
        stack_ref, weight_ref = take(2)
        far, near, mid = take(chunks), take(chunks), take(chunks)
        finish(chunks, seq, norm, att, stack_ref, weight_ref, far, near, mid, *refs)

    return pl.pallas_call(
        kernel,
        in_specs=[vmem] * (4 * chunks + 2),
        out_specs=[vmem] * 3,
        out_shape=[
            jax.ShapeDtypeStruct((rows, width), BF16),
            jax.ShapeDtypeStruct((2, rows, depth), BF16),
            jax.ShapeDtypeStruct((depth, piece), F32),
        ],
        scratch_shapes=[
            pltpu.VMEM(rim, BF16),
            pltpu.VMEM(rim, BF16),
            pltpu.VMEM(rim, BF16),
            pltpu.VMEM((4, depth, piece), BF16),
            pltpu.VMEM((4, depth, piece), BF16),
            pltpu.VMEM((4, depth, piece), F32),
            pltpu.VMEM((2, depth, piece), BF16),
            pltpu.VMEM((2, depth, piece), BF16),
            pltpu.VMEM((depth, piece), BF16),
            pltpu.VMEM((depth, piece), BF16),
            pltpu.VMEM((2, rows, width), BF16),
            pltpu.VMEM((2, rows, width), BF16),
            pltpu.VMEM((rows, width), F32),
            pltpu.VMEM((rows, width), F32),
            pltpu.VMEM((rows, width), BF16),
            pltpu.VMEM((rows, width), BF16),
            sem((chunks,)), sem((chunks,)), sem((chunks,)), sem((chunks,)),
            sem((4,)), sem((4,)), sem((2,)), sem((2,)), sem((1,)), sem((1,)),
            sem((2,)), sem((2,)), sem((1,)), sem((1,)),
        ],
        compiler_params=pltpu.CompilerParams(
            collective_id=0, has_side_effects=True, vmem_limit_bytes=60 << 20
        ),
        cost_estimate=pl.CostEstimate(
            flops=4 * rows * depth * width * 4, bytes_accessed=40 << 20, transcendentals=0
        ),
    )(*atts, stacked, weight, *fars, *nears, *mids)


def local(queries, key_rows, value_rows, out_weight, cotangent, neighbours):
    rows, columns = queries.shape
    heads = columns // HD
    tiles = rows // TILE
    seq, head = lax.axis_size("seq"), lax.axis_size("head")
    s, h = lax.axis_index("seq"), lax.axis_index("head")
    paired = head == 4 and seq == 8
    width = cotangent.shape[1]
    piece = width * head // seq
    norm = 1.0 / math.sqrt(rows * seq)
    chunks = 2
    per = heads // chunks

    halos = []
    for n in range(chunks):
        cut = slice(n * per * HD, (n + 1) * per * HD)
        kv = jnp.stack([key_rows[:, cut], value_rows[:, cut]])
        near = swap(kv, "seq", 1)
        far = shift(near, "seq", 2)
        halos.append((far, near))

    if paired:
        shards = [cotangent, swap(cotangent, "head", 1), swap(cotangent, "head", 2)]
        shards.append(swap(shards[2], "head", 1))
        weights = [
            lax.dynamic_slice_in_dim(out_weight, (h ^ r) * width, width, 1) for r in range(4)
        ]
        grad_attention = sum(dot_nt(a, b) for a, b in zip(shards, weights)).astype(BF16)
    else:
        full = lax.all_gather(cotangent, "head", axis=1, tiled=True)
        grad_attention = dot_nt(full, out_weight).astype(BF16)

    first = s * tiles - REACH
    alive = neighbours >= 0
    index = jnp.where(alive, neighbours - first, 0)
    span = tiles + REACH
    odd = s % 2 == 1
    turned = jnp.where(index < REACH, index + span, jnp.where(index >= span, index - span, index))
    place = jnp.where(odd, turned, index).reshape(-1).astype(jnp.int32)
    count = jnp.sum(alive, axis=1).astype(jnp.int32)

    atts, dqs, mids, fars, nears = [], [], [], [], []
    for n in range(chunks):
        far, near = halos[n]
        att, dq, mid, rim_far, rim_near = attention_call(
            place, count, queries, grad_attention, key_rows, value_rows, far, near, n * per, per
        )
        atts.append(att)
        dqs.append(dq)
        mids.append(mid)
        fars.append(rim_far)
        nears.append(rim_near)

    grad_queries = jnp.concatenate(dqs, axis=1)
    if paired:
        projected, dkv, grad_weight = finish_call(
            atts, jnp.stack(shards), out_weight, fars, nears, mids, seq, norm
        )
        return (projected, grad_queries, dkv[0], dkv[1], grad_weight)

    dks, dvs = [], []
    for n in range(chunks):
        relayed = shift(fars[n], "seq", -2)
        back = swap((nears[n] + relayed.astype(F32)).astype(BF16), "seq", 1)
        done = (mids[n] + back.astype(F32)).astype(BF16)
        dks.append(done[0])
        dvs.append(done[1])
    attention = jnp.concatenate(atts, axis=1)
    projected = lax.psum_scatter(
        dot_nn(attention, out_weight).astype(BF16), "head", scatter_dimension=1, tiled=True
    )
    grad_weight = (
        lax.psum_scatter(
            dot_tn(attention, full).astype(BF16), "seq", scatter_dimension=1, tiled=True
        ).astype(F32)
        * norm
    )
    return (
        projected,
        grad_queries,
        jnp.concatenate(dks, axis=1),
        jnp.concatenate(dvs, axis=1),
        grad_weight,
    )


def solution(mesh):
    both = P("seq", "head")
    return jax.shard_map(
        local,
        mesh=mesh,
        in_specs=(both, both, both, P("head", None), both, P("seq", None)),
        out_specs=(both, both, both, both, P("head", "seq")),
        check_vma=False,
    )
```

```python
import functools
import math

import jax
import jax.numpy as jnp
from jax import lax
from jax.experimental import pallas as pl
from jax.experimental.pallas import tpu as pltpu
from jax.sharding import PartitionSpec as P

HD = 128
TILE = 384
REACH = 2
SLOTS = 4
RIM = REACH * TILE
F32 = jnp.float32
BF16 = jnp.bfloat16


def dot_nt(a, b):
    return lax.dot_general(a, b, (((1,), (1,)), ((), ())), preferred_element_type=F32)


def dot_nn(a, b):
    return lax.dot_general(a, b, (((1,), (0,)), ((), ())), preferred_element_type=F32)


def dot_tn(a, b):
    return lax.dot_general(a, b, (((0,), (0,)), ((), ())), preferred_element_type=F32)


def fold(op, x):
    out = x[:, :HD]
    for i in range(1, x.shape[1] // HD):
        out = op(out, x[:, i * HD : (i + 1) * HD])
    return out


def attend(rows, tiles, place, count, q, g, km, vm, far, near, att, dq, mid, rim_far, rim_near, kx, vx, dk, dv, scr):
    t = pl.program_id(1)
    scale = 1.0 / math.sqrt(HD)
    c = scale * math.log2(math.e)
    hi = RIM + rows

    @pl.when(t == 0)
    def _():
        kx[:RIM] = far[0]
        kx[RIM:hi] = km[...]
        kx[hi:] = near[0]
        vx[:RIM] = far[1]
        vx[RIM:hi] = vm[...]
        vx[hi:] = near[1]
        dk[...] = jnp.zeros_like(dk)
        dv[...] = jnp.zeros_like(dv)

    live = count[t]
    qv = q[...]
    gv = g[...]

    def at(j):
        return pl.ds(pl.multiple_of(place[t * SLOTS + j] * TILE, TILE), TILE)

    def score(j, m):
        s = dot_nt(qv, kx[at(j), :])
        scr[j] = s
        return jnp.maximum(m, fold(jnp.maximum, s))

    m = lax.fori_loop(0, live, score, jnp.full((TILE, HD), -3e38, F32))
    m = jnp.max(m, axis=1, keepdims=True)

    def soft(j, carry):
        total, acc = carry
        e = jnp.exp2((scr[j] - m) * c)
        scr[j] = e
        return total + fold(jnp.add, e), acc + dot_nn(e.astype(BF16), vx[at(j), :])

    zero = jnp.zeros((TILE, HD), F32)
    total, acc = lax.fori_loop(0, live, soft, (zero, zero))
    inv = 1.0 / jnp.sum(total, axis=1, keepdims=True)
    out = (acc * inv).astype(BF16)
    att[...] = out
    delta = jnp.sum(gv.astype(F32) * out.astype(F32), axis=1, keepdims=True)

    def back(j, acc):
        here = at(j)
        k = kx[here, :]
        p = scr[j] * inv
        ds = (p * (dot_nt(gv, vx[here, :]) - delta)).astype(BF16)
        dv[here, :] += dot_tn(p.astype(BF16), gv)
        dk[here, :] += dot_tn(ds, qv)
        return acc + dot_nn(ds, k)

    dq[...] = (lax.fori_loop(0, live, back, zero) * scale).astype(BF16)

    @pl.when(t == tiles - 1)
    def _():
        rim_far[0] = (dk[:RIM] * scale).astype(BF16)
        rim_far[1] = dv[:RIM].astype(BF16)
        mid[0] = dk[RIM:hi] * scale
        mid[1] = dv[RIM:hi]
        rim_near[0] = dk[hi:] * scale
        rim_near[1] = dv[hi:]


def attention_call(place, count, q, g, k, v, far, near, first, heads):
    rows = q.shape[0]
    tiles = rows // TILE
    ext = rows + 2 * RIM
    cols = heads * HD
    tile_in = pl.BlockSpec((TILE, HD), lambda h, t, *_: (t, first + h))
    slab_in = pl.BlockSpec((rows, HD), lambda h, t, *_: (0, first + h))
    rim = pl.BlockSpec((2, RIM, HD), lambda h, t, *_: (0, 0, h))
    tile_out = pl.BlockSpec((TILE, HD), lambda h, t, *_: (t, h))
    mid = pl.BlockSpec((2, rows, HD), lambda h, t, *_: (0, 0, h))
    pairs = heads * tiles * SLOTS
    return pl.pallas_call(
        functools.partial(attend, rows, tiles),
        grid_spec=pltpu.PrefetchScalarGridSpec(
            num_scalar_prefetch=2,
            grid=(heads, tiles),
            in_specs=[tile_in, tile_in, slab_in, slab_in, rim, rim],
            out_specs=[tile_out, tile_out, mid, rim, rim],
            scratch_shapes=[
                pltpu.VMEM((ext, HD), BF16),
                pltpu.VMEM((ext, HD), BF16),
                pltpu.VMEM((ext, HD), F32),
                pltpu.VMEM((ext, HD), F32),
                pltpu.VMEM((SLOTS, TILE, TILE), F32),
            ],
        ),
        out_shape=[
            jax.ShapeDtypeStruct((rows, cols), BF16),
            jax.ShapeDtypeStruct((rows, cols), BF16),
            jax.ShapeDtypeStruct((2, rows, cols), F32),
            jax.ShapeDtypeStruct((2, RIM, cols), BF16),
            jax.ShapeDtypeStruct((2, RIM, cols), F32),
        ],
        compiler_params=pltpu.CompilerParams(
            dimension_semantics=("arbitrary", "arbitrary"), vmem_limit_bytes=40 << 20
        ),
        cost_estimate=pl.CostEstimate(
            flops=pairs * 12 * TILE * TILE * HD,
            bytes_accessed=rows * cols * 40,
            transcendentals=pairs * TILE * TILE,
        ),
    )(place, count, q, g, k, v, far, near)


def swap(x, axis, bit):
    return lax.ppermute(x, axis, [(i, i ^ bit) for i in range(lax.axis_size(axis))])


def shift(x, axis, even_step):
    size = lax.axis_size(axis)
    pairs = [(i, i + (even_step if i % 2 == 0 else -even_step)) for i in range(size)]
    return lax.ppermute(x, axis, [(i, j) for i, j in pairs if 0 <= j < size])


def away_terms(turned, side, att, cols, out):
    out[0] = dot_tn(att[...], cols[0]).astype(BF16)


def away_call(turned, side, att, stacked, piece):
    rows, part = att.shape
    return pl.pallas_call(
        away_terms,
        grid_spec=pltpu.PrefetchScalarGridSpec(
            num_scalar_prefetch=2,
            grid=(4,),
            in_specs=[
                pl.BlockSpec((rows, part), lambda k, *_: (0, 0)),
                pl.BlockSpec((1, rows, piece), lambda k, t, x: (t[k], 0, 1 - x[0])),
            ],
            out_specs=pl.BlockSpec((1, part, piece), lambda k, *_: (k, 0, 0)),
        ),
        out_shape=jax.ShapeDtypeStruct((4, part, piece), BF16),
        compiler_params=pltpu.CompilerParams(dimension_semantics=("arbitrary",)),
        cost_estimate=pl.CostEstimate(
            flops=8 * rows * part * piece, bytes_accessed=rows * piece * 12, transcendentals=0
        ),
    )(turned, side, att, stacked)


MESH = pl.DeviceIdType.MESH


def finish(
    chunks, seq, norm,
    att, stacked, weight, rim_far, rim_near, mid, relay, crossed,
    projected, dk, dv, grad_weight,
    far_in, near_out, near_in, gw_out, gw_in, gw_sum, two_out, two_in, four_out, four_in,
    core_out, core_in, mine, theirs, y_out, y_in,
    far_s, far_r, near_s, near_r, gw_s, gw_r, two_s, two_r, four_s, four_r, core_s, core_r, y_s, y_r,
):
    s, h = lax.axis_index("seq"), lax.axis_index("head")
    x, z0, z1 = s % 2, (s // 2) % 2, (s // 4) % 2
    h0, h1 = h % 2, (h // 2) % 2
    beside = (s + 1 - 2 * x, h)
    hop2 = (s + 2 - 4 * z0, h)
    hop4 = (s + 4 - 8 * z1, h)
    mate = (s, h + 1 - 2 * h0)
    across = (s, h + 2 - 4 * h1)
    below, above = s >= 2, s + 2 < seq
    width = projected.shape[1]
    piece = grad_weight.shape[1]
    part = att[0].shape[1]

    def send(src, dst, sems, semr, i, dev):
        return pltpu.make_async_remote_copy(
            src_ref=src, dst_ref=dst, send_sem=sems.at[i], recv_sem=semr.at[i],
            device_id=dev, device_id_type=MESH,
        )

    barrier = pltpu.get_barrier_semaphore()
    for dev in (beside, hop4, mate, across):
        pl.semaphore_signal(barrier, inc=1, device_id=dev, device_id_type=MESH)

    @pl.when(below)
    def _():
        pl.semaphore_signal(barrier, inc=1, device_id=(s - 2, h), device_id_type=MESH)

    @pl.when(above)
    def _():
        pl.semaphore_signal(barrier, inc=1, device_id=(s + 2, h), device_id_type=MESH)

    pl.semaphore_wait(barrier, 4 + (s + seq - 2) // seq + (2 * seq - 3 - s) // seq)

    down = s - 2 + 4 * x
    sends_far = (down >= 0) & (down < seq)
    up = s + 2 - 4 * x
    gets_far = (up >= 0) & (up < seq)
    nears = [send(near_out.at[c], near_in.at[c], near_s, near_r, c, beside) for c in range(chunks)]
    far = send(rim_far[1], far_in, far_s, far_r, 0, (down, h))

    @pl.when(sends_far)
    def _():
        far.start()

    for i in range(2):
        near_out[0, i] = (rim_near[0][i] + relay[i].astype(F32)).astype(BF16)
    nears[0].start()

    def columns(k, side):
        r = (h0 + z0 + k % 2) % 2 + 2 * ((h1 + z1 + k // 2) % 2)
        return stacked[r, :, pl.ds(pl.multiple_of(side * piece, piece), piece)]

    gws = []
    for k in (1, 3, 2, 0):
        cot = columns(k, 1 - x)
        gw_out[k] = dot_tn(att[1][...], cot).astype(BF16)
        gws.append(send(gw_out.at[k], gw_in.at[k], gw_s, gw_r, k, beside))
        gws[-1].start()

    def share(r):
        b0, b1 = (h0 + r % 2) % 2, (h1 + r // 2) % 2
        at = pl.ds(pl.multiple_of((b0 + 2 * b1) * width, width), width)
        total = dot_nn(att[0][...], weight[:part, at])
        for c in range(1, chunks):
            total += dot_nn(att[c][...], weight[c * part : (c + 1) * part, at])
        return total

    cores = []
    for i, r in enumerate((3, 1)):
        core_out[i] = share(r).astype(BF16)
        cores.append(send(core_out.at[i], core_in.at[i], core_s, core_r, i, mate))
        cores[-1].start()
    theirs[...] = share(2)
    cores[0].wait_recv()
    y_out[...] = (theirs[...] + core_in[0].astype(F32)).astype(BF16)
    ys = send(y_out, y_in, y_s, y_r, 0, across)
    ys.start()

    @pl.when(gets_far)
    def _():
        far.wait_recv()
        for i in range(2):
            near_out[1, i] = (rim_near[1][i] + far_in[i].astype(F32)).astype(BF16)

    @pl.when(jnp.logical_not(gets_far))
    def _():
        for i in range(2):
            near_out[1, i] = rim_near[1][i].astype(BF16)

    nears[1].start()

    for k in range(4):
        cot = columns(k, x)
        for c in range(chunks):
            gw_sum[k, c * part : (c + 1) * part] = dot_tn(att[c][...], cot)
        gw_sum[k, :part] += crossed[k].astype(F32)
    mine[...] = share(0)
    cores[1].wait_recv()
    mine[...] += core_in[1].astype(F32)

    twos = []
    for i, k in enumerate((1, 3)):
        gws[i].wait_recv()
        gw_sum[k, part:] += gw_in[k].astype(F32)
        two_out[i] = gw_sum[k].astype(BF16)
        twos.append(send(two_out.at[i], two_in.at[i], two_s, two_r, i, hop2))
    twos[1].start()
    twos[0].start()
    gws[2].wait_recv()
    gw_sum[2, part:] += gw_in[2].astype(F32)
    gws[3].wait_recv()
    gw_sum[0, part:] += gw_in[0].astype(F32)
    twos[1].wait_recv()
    four_out[...] = (gw_sum[2] + two_in[1].astype(F32)).astype(BF16)
    four = send(four_out, four_in, four_s, four_r, 0, hop4)
    four.start()
    twos[0].wait_recv()
    gw_sum[0] += two_in[0].astype(F32)

    ys.wait_recv()
    projected[...] = (mine[...] + y_in[...].astype(F32)).astype(BF16)
    four.wait_recv()
    grad_weight[...] = (gw_sum[0] + four_in[...].astype(F32)) * norm
    for c in range(chunks):
        nears[c].wait_recv()
        for i, out in enumerate((dk, dv)):
            out[:, c * part : (c + 1) * part] = (mid[c][i] + near_in[c, i].astype(F32)).astype(BF16)

    @pl.when(sends_far)
    def _():
        far.wait_send()

    for copy in gws + cores + nears + twos + [ys, four]:
        copy.wait_send()


def finish_call(atts, stacked, weight, fars, nears, mids, relay, crossed, seq, norm):
    chunks = len(atts)
    rows, part = atts[0].shape
    depth = chunks * part
    width = stacked.shape[2]
    piece = width * 4 // seq
    vmem = pl.BlockSpec(memory_space=pltpu.VMEM)
    rim = (chunks, 2, RIM, part)
    sem = pltpu.SemaphoreType.DMA

    def kernel(*refs):
        refs = list(refs)

        def take(n):
            got = refs[:n]
            del refs[:n]
            return got

        att = take(chunks)
        stack_ref, weight_ref = take(2)
        far, near, mid = take(chunks), take(chunks), take(chunks)
        finish(chunks, seq, norm, att, stack_ref, weight_ref, far, near, mid, *refs)

    return pl.pallas_call(
        kernel,
        in_specs=[vmem] * (4 * chunks + 4),
        out_specs=[vmem] * 4,
        out_shape=[
            jax.ShapeDtypeStruct((rows, width), BF16),
            jax.ShapeDtypeStruct((rows, depth), BF16),
            jax.ShapeDtypeStruct((rows, depth), BF16),
            jax.ShapeDtypeStruct((depth, piece), F32),
        ],
        scratch_shapes=[
            pltpu.VMEM((2, RIM, part), BF16),
            pltpu.VMEM(rim, BF16),
            pltpu.VMEM(rim, BF16),
            pltpu.VMEM((4, part, piece), BF16),
            pltpu.VMEM((4, part, piece), BF16),
            pltpu.VMEM((4, depth, piece), F32),
            pltpu.VMEM((2, depth, piece), BF16),
            pltpu.VMEM((2, depth, piece), BF16),
            pltpu.VMEM((depth, piece), BF16),
            pltpu.VMEM((depth, piece), BF16),
            pltpu.VMEM((2, rows, width), BF16),
            pltpu.VMEM((2, rows, width), BF16),
            pltpu.VMEM((rows, width), F32),
            pltpu.VMEM((rows, width), F32),
            pltpu.VMEM((rows, width), BF16),
            pltpu.VMEM((rows, width), BF16),
            sem((1,)), sem((1,)), sem((chunks,)), sem((chunks,)),
            sem((4,)), sem((4,)), sem((2,)), sem((2,)), sem((1,)), sem((1,)),
            sem((2,)), sem((2,)), sem((1,)), sem((1,)),
        ],
        compiler_params=pltpu.CompilerParams(
            collective_id=0, has_side_effects=True, vmem_limit_bytes=60 << 20
        ),
        cost_estimate=pl.CostEstimate(
            flops=4 * rows * depth * width * 4, bytes_accessed=40 << 20, transcendentals=0
        ),
    )(*atts, stacked, weight, *fars, *nears, *mids, relay, crossed)


def local(queries, key_rows, value_rows, out_weight, cotangent, neighbours):
    rows, columns = queries.shape
    heads = columns // HD
    tiles = rows // TILE
    seq, head = lax.axis_size("seq"), lax.axis_size("head")
    s, h = lax.axis_index("seq"), lax.axis_index("head")
    paired = head == 4 and seq == 8
    width = cotangent.shape[1]
    piece = width * head // seq
    norm = 1.0 / math.sqrt(rows * seq)
    chunks = 2
    per = heads // chunks

    halos = []
    for n in range(chunks):
        cut = slice(n * per * HD, (n + 1) * per * HD)
        kv = jnp.stack([key_rows[:, cut], value_rows[:, cut]])
        near = swap(kv, "seq", 1)
        far = shift(near, "seq", 2)
        halos.append((far, near))

    if paired:
        shards = [cotangent, swap(cotangent, "head", 1), swap(cotangent, "head", 2)]
        shards.append(swap(shards[2], "head", 1))
        weights = [
            lax.dynamic_slice_in_dim(out_weight, (h ^ r) * width, width, 1) for r in range(4)
        ]
        grad_attention = sum(dot_nt(a, b) for a, b in zip(shards, weights)).astype(BF16)
    else:
        full = lax.all_gather(cotangent, "head", axis=1, tiled=True)
        grad_attention = dot_nt(full, out_weight).astype(BF16)

    first = s * tiles - REACH
    alive = neighbours >= 0
    index = jnp.where(alive, neighbours - first, 0)
    span = tiles + REACH
    odd = s % 2 == 1
    turned = jnp.where(index < REACH, index + span, jnp.where(index >= span, index - span, index))
    place = jnp.where(odd, turned, index).reshape(-1).astype(jnp.int32)
    count = jnp.sum(alive, axis=1).astype(jnp.int32)

    atts, dqs, mids, fars, nears = [], [], [], [], []
    if paired:
        stacked = jnp.stack(shards)
        turned = ((h ^ (s // 2)) ^ jnp.arange(4, dtype=jnp.int32)).astype(jnp.int32)
        side = (s % 2).astype(jnp.int32).reshape(1)
        place, stacked = lax.optimization_barrier((place, stacked))
    for n in range(chunks):
        far, near = halos[n]
        if n == 1 and paired:
            place, relay = lax.optimization_barrier((place, fars[0]))
            relay = shift(relay, "seq", -2)
            away = away_call(turned, side, atts[0], stacked, piece)
            place, away = lax.optimization_barrier((place, away))
            crossed = swap(away, "seq", 1)
        att, dq, mid, rim_far, rim_near = attention_call(
            place, count, queries, grad_attention, key_rows, value_rows, far, near, n * per, per
        )
        atts.append(att)
        dqs.append(dq)
        mids.append(mid)
        fars.append(rim_far)
        nears.append(rim_near)

    grad_queries = jnp.concatenate(dqs, axis=1)
    if paired:
        projected, grad_keys, grad_values, grad_weight = finish_call(
            atts, stacked, out_weight, fars, nears, mids, relay, crossed, seq, norm
        )
        return (projected, grad_queries, grad_keys, grad_values, grad_weight)

    dks, dvs = [], []
    for n in range(chunks):
        relayed = shift(fars[n], "seq", -2)
        back = swap((nears[n] + relayed.astype(F32)).astype(BF16), "seq", 1)
        done = (mids[n] + back.astype(F32)).astype(BF16)
        dks.append(done[0])
        dvs.append(done[1])
    attention = jnp.concatenate(atts, axis=1)
    projected = lax.psum_scatter(
        dot_nn(attention, out_weight).astype(BF16), "head", scatter_dimension=1, tiled=True
    )
    grad_weight = (
        lax.psum_scatter(
            dot_tn(attention, full).astype(BF16), "seq", scatter_dimension=1, tiled=True
        ).astype(F32)
        * norm
    )
    return (
        projected,
        grad_queries,
        jnp.concatenate(dks, axis=1),
        jnp.concatenate(dvs, axis=1),
        grad_weight,
    )


def solution(mesh):
    both = P("seq", "head")
    return jax.shard_map(
        local,
        mesh=mesh,
        in_specs=(both, both, both, P("head", None), both, P("seq", None)),
        out_specs=(both, both, both, both, P("head", "seq")),
        check_vma=False,
    )
```

```python
import functools
import math

import jax
import jax.numpy as jnp
from jax import lax
from jax.experimental import pallas as pl
from jax.experimental.pallas import tpu as pltpu
from jax.sharding import PartitionSpec as P

HD = 128
TILE = 384
REACH = 2
SLOTS = 4
RIM = REACH * TILE
F32 = jnp.float32
BF16 = jnp.bfloat16


def dot_nt(a, b):
    return lax.dot_general(a, b, (((1,), (1,)), ((), ())), preferred_element_type=F32)


def dot_nn(a, b):
    return lax.dot_general(a, b, (((1,), (0,)), ((), ())), preferred_element_type=F32)


def dot_tn(a, b):
    return lax.dot_general(a, b, (((0,), (0,)), ((), ())), preferred_element_type=F32)


def fold(op, x):
    out = x[:, :HD]
    for i in range(1, x.shape[1] // HD):
        out = op(out, x[:, i * HD : (i + 1) * HD])
    return out


def attend(rows, tiles, place, count, q, g, km, vm, far, near, att, dq, mid, rim_far, rim_near, kx, vx, dk, dv, scr):
    t = pl.program_id(1)
    scale = 1.0 / math.sqrt(HD)
    c = scale * math.log2(math.e)
    hi = RIM + rows

    @pl.when(t == 0)
    def _():
        kx[:RIM] = far[0]
        kx[RIM:hi] = km[...]
        kx[hi:] = near[0]
        vx[:RIM] = far[1]
        vx[RIM:hi] = vm[...]
        vx[hi:] = near[1]
        dk[...] = jnp.zeros_like(dk)
        dv[...] = jnp.zeros_like(dv)

    live = count[t]
    qv = q[...]
    gv = g[...]

    def at(j):
        return pl.ds(pl.multiple_of(place[t * SLOTS + j] * TILE, TILE), TILE)

    def slots(step, carry):
        for j in range(SLOTS):
            carry = step(j, carry)
        return carry

    def score(j, m):
        s = dot_nt(qv, kx[at(j), :])
        if j:
            s = jnp.where(j < live, s, -1e30)
        scr[j] = s
        return jnp.maximum(m, fold(jnp.maximum, s))

    m = slots(score, jnp.full((TILE, HD), -3e38, F32))
    m = jnp.max(m, axis=1, keepdims=True)

    def soft(j, carry):
        total, acc = carry
        e = jnp.exp2((scr[j] - m) * c)
        scr[j] = e
        return total + fold(jnp.add, e), acc + dot_nn(e.astype(BF16), vx[at(j), :])

    zero = jnp.zeros((TILE, HD), F32)
    total, acc = slots(soft, (zero, zero))
    inv = 1.0 / jnp.sum(total, axis=1, keepdims=True)
    out = (acc * inv).astype(BF16)
    att[...] = out
    delta = jnp.sum(gv.astype(F32) * out.astype(F32), axis=1, keepdims=True)

    def back(j, acc):
        here = at(j)
        k = kx[here, :]
        p = scr[j] * inv
        ds = (p * (dot_nt(gv, vx[here, :]) - delta)).astype(BF16)
        dv[here, :] += dot_tn(p.astype(BF16), gv)
        dk[here, :] += dot_tn(ds, qv)
        return acc + dot_nn(ds, k)

    dq[...] = (slots(back, zero) * scale).astype(BF16)

    @pl.when(t == tiles - 1)
    def _():
        rim_far[0] = (dk[:RIM] * scale).astype(BF16)
        rim_far[1] = dv[:RIM].astype(BF16)
        mid[0] = dk[RIM:hi] * scale
        mid[1] = dv[RIM:hi]
        rim_near[0] = dk[hi:] * scale
        rim_near[1] = dv[hi:]


def attention_call(place, count, q, g, k, v, far, near, first, heads):
    rows = q.shape[0]
    tiles = rows // TILE
    ext = rows + 2 * RIM
    cols = heads * HD
    tile_in = pl.BlockSpec((TILE, HD), lambda h, t, *_: (t, first + h))
    slab_in = pl.BlockSpec((rows, HD), lambda h, t, *_: (0, first + h))
    rim = pl.BlockSpec((2, RIM, HD), lambda h, t, *_: (0, 0, h))
    tile_out = pl.BlockSpec((TILE, HD), lambda h, t, *_: (t, h))
    mid = pl.BlockSpec((2, rows, HD), lambda h, t, *_: (0, 0, h))
    pairs = heads * tiles * SLOTS
    return pl.pallas_call(
        functools.partial(attend, rows, tiles),
        grid_spec=pltpu.PrefetchScalarGridSpec(
            num_scalar_prefetch=2,
            grid=(heads, tiles),
            in_specs=[tile_in, tile_in, slab_in, slab_in, rim, rim],
            out_specs=[tile_out, tile_out, mid, rim, rim],
            scratch_shapes=[
                pltpu.VMEM((ext, HD), BF16),
                pltpu.VMEM((ext, HD), BF16),
                pltpu.VMEM((ext, HD), F32),
                pltpu.VMEM((ext, HD), F32),
                pltpu.VMEM((SLOTS, TILE, TILE), F32),
            ],
        ),
        out_shape=[
            jax.ShapeDtypeStruct((rows, cols), BF16),
            jax.ShapeDtypeStruct((rows, cols), BF16),
            jax.ShapeDtypeStruct((2, rows, cols), F32),
            jax.ShapeDtypeStruct((2, RIM, cols), BF16),
            jax.ShapeDtypeStruct((2, RIM, cols), F32),
        ],
        compiler_params=pltpu.CompilerParams(
            dimension_semantics=("arbitrary", "arbitrary"), vmem_limit_bytes=40 << 20
        ),
        cost_estimate=pl.CostEstimate(
            flops=pairs * 12 * TILE * TILE * HD,
            bytes_accessed=rows * cols * 40,
            transcendentals=pairs * TILE * TILE,
        ),
    )(place, count, q, g, k, v, far, near)


def swap(x, axis, bit):
    return lax.ppermute(x, axis, [(i, i ^ bit) for i in range(lax.axis_size(axis))])


def shift(x, axis, even_step):
    size = lax.axis_size(axis)
    pairs = [(i, i + (even_step if i % 2 == 0 else -even_step)) for i in range(size)]
    return lax.ppermute(x, axis, [(i, j) for i, j in pairs if 0 <= j < size])


def away_terms(turned, side, att, cols, out):
    out[0] = dot_tn(att[...], cols[0]).astype(BF16)


def away_call(turned, side, att, stacked, piece):
    rows, part = att.shape
    return pl.pallas_call(
        away_terms,
        grid_spec=pltpu.PrefetchScalarGridSpec(
            num_scalar_prefetch=2,
            grid=(4,),
            in_specs=[
                pl.BlockSpec((rows, part), lambda k, *_: (0, 0)),
                pl.BlockSpec((1, rows, piece), lambda k, t, x: (t[k], 0, 1 - x[0])),
            ],
            out_specs=pl.BlockSpec((1, part, piece), lambda k, *_: (k, 0, 0)),
        ),
        out_shape=jax.ShapeDtypeStruct((4, part, piece), BF16),
        compiler_params=pltpu.CompilerParams(dimension_semantics=("arbitrary",)),
        cost_estimate=pl.CostEstimate(
            flops=8 * rows * part * piece, bytes_accessed=rows * piece * 12, transcendentals=0
        ),
    )(turned, side, att, stacked)


MESH = pl.DeviceIdType.MESH


def finish(
    chunks, seq, norm,
    att, stacked, weight, rim_far, rim_near, mid, relay, crossed,
    projected, dk, dv, grad_weight,
    far_in, near_out, near_in, gw_out, gw_in, gw_sum, two_out, two_in, four_out, four_in,
    core_out, core_in, mine, theirs, y_out, y_in,
    far_s, far_r, near_s, near_r, gw_s, gw_r, two_s, two_r, four_s, four_r, core_s, core_r, y_s, y_r,
):
    s, h = lax.axis_index("seq"), lax.axis_index("head")
    x, z0, z1 = s % 2, (s // 2) % 2, (s // 4) % 2
    h0, h1 = h % 2, (h // 2) % 2
    beside = (s + 1 - 2 * x, h)
    hop2 = (s + 2 - 4 * z0, h)
    hop4 = (s + 4 - 8 * z1, h)
    mate = (s, h + 1 - 2 * h0)
    across = (s, h + 2 - 4 * h1)
    below, above = s >= 2, s + 2 < seq
    width = projected.shape[1]
    piece = grad_weight.shape[1]
    part = att[0].shape[1]

    def send(src, dst, sems, semr, i, dev):
        return pltpu.make_async_remote_copy(
            src_ref=src, dst_ref=dst, send_sem=sems.at[i], recv_sem=semr.at[i],
            device_id=dev, device_id_type=MESH,
        )

    barrier = pltpu.get_barrier_semaphore()
    for dev in (beside, hop4, mate, across):
        pl.semaphore_signal(barrier, inc=1, device_id=dev, device_id_type=MESH)

    @pl.when(below)
    def _():
        pl.semaphore_signal(barrier, inc=1, device_id=(s - 2, h), device_id_type=MESH)

    @pl.when(above)
    def _():
        pl.semaphore_signal(barrier, inc=1, device_id=(s + 2, h), device_id_type=MESH)

    pl.semaphore_wait(barrier, 4 + (s + seq - 2) // seq + (2 * seq - 3 - s) // seq)

    down = s - 2 + 4 * x
    sends_far = (down >= 0) & (down < seq)
    up = s + 2 - 4 * x
    gets_far = (up >= 0) & (up < seq)
    nears = [send(near_out.at[c], near_in.at[c], near_s, near_r, c, beside) for c in range(chunks)]
    far = send(rim_far[1], far_in, far_s, far_r, 0, (down, h))

    @pl.when(sends_far)
    def _():
        far.start()

    for i in range(2):
        near_out[0, i] = (rim_near[0][i] + relay[i].astype(F32)).astype(BF16)
    nears[0].start()

    def columns(k, side):
        r = (h0 + z0 + k % 2) % 2 + 2 * ((h1 + z1 + k // 2) % 2)
        return stacked[r, :, pl.ds(pl.multiple_of(side * piece, piece), piece)]

    gws = []
    for k in (1, 3, 2, 0):
        cot = columns(k, 1 - x)
        gw_out[k] = dot_tn(att[1][...], cot).astype(BF16)
        gws.append(send(gw_out.at[k], gw_in.at[k], gw_s, gw_r, k, beside))
        gws[-1].start()

    def share(r):
        b0, b1 = (h0 + r % 2) % 2, (h1 + r // 2) % 2
        at = pl.ds(pl.multiple_of((b0 + 2 * b1) * width, width), width)
        total = dot_nn(att[0][...], weight[:part, at])
        for c in range(1, chunks):
            total += dot_nn(att[c][...], weight[c * part : (c + 1) * part, at])
        return total

    cores = []
    for i, r in enumerate((3, 1)):
        core_out[i] = share(r).astype(BF16)
        cores.append(send(core_out.at[i], core_in.at[i], core_s, core_r, i, mate))
        cores[-1].start()
    theirs[...] = share(2)
    cores[0].wait_recv()
    y_out[...] = (theirs[...] + core_in[0].astype(F32)).astype(BF16)
    ys = send(y_out, y_in, y_s, y_r, 0, across)
    ys.start()

    @pl.when(gets_far)
    def _():
        far.wait_recv()
        for i in range(2):
            near_out[1, i] = (rim_near[1][i] + far_in[i].astype(F32)).astype(BF16)

    @pl.when(jnp.logical_not(gets_far))
    def _():
        for i in range(2):
            near_out[1, i] = rim_near[1][i].astype(BF16)

    nears[1].start()

    for k in range(4):
        cot = columns(k, x)
        for c in range(chunks):
            gw_sum[k, c * part : (c + 1) * part] = dot_tn(att[c][...], cot)
        gw_sum[k, :part] += crossed[k].astype(F32)
    mine[...] = share(0)
    cores[1].wait_recv()
    mine[...] += core_in[1].astype(F32)

    twos = []
    for i, k in enumerate((1, 3)):
        gws[i].wait_recv()
        gw_sum[k, part:] += gw_in[k].astype(F32)
        two_out[i] = gw_sum[k].astype(BF16)
        twos.append(send(two_out.at[i], two_in.at[i], two_s, two_r, i, hop2))
    twos[1].start()
    twos[0].start()
    gws[2].wait_recv()
    gw_sum[2, part:] += gw_in[2].astype(F32)
    gws[3].wait_recv()
    gw_sum[0, part:] += gw_in[0].astype(F32)
    twos[1].wait_recv()
    four_out[...] = (gw_sum[2] + two_in[1].astype(F32)).astype(BF16)
    four = send(four_out, four_in, four_s, four_r, 0, hop4)
    four.start()
    twos[0].wait_recv()
    gw_sum[0] += two_in[0].astype(F32)

    ys.wait_recv()
    projected[...] = (mine[...] + y_in[...].astype(F32)).astype(BF16)
    four.wait_recv()
    grad_weight[...] = (gw_sum[0] + four_in[...].astype(F32)) * norm
    for c in range(chunks):
        nears[c].wait_recv()
        for i, out in enumerate((dk, dv)):
            out[:, c * part : (c + 1) * part] = (mid[c][i] + near_in[c, i].astype(F32)).astype(BF16)

    @pl.when(sends_far)
    def _():
        far.wait_send()

    for copy in gws + cores + nears + twos + [ys, four]:
        copy.wait_send()


def finish_call(atts, stacked, weight, fars, nears, mids, relay, crossed, seq, norm):
    chunks = len(atts)
    rows, part = atts[0].shape
    depth = chunks * part
    width = stacked.shape[2]
    piece = width * 4 // seq
    vmem = pl.BlockSpec(memory_space=pltpu.VMEM)
    rim = (chunks, 2, RIM, part)
    sem = pltpu.SemaphoreType.DMA

    def kernel(*refs):
        refs = list(refs)

        def take(n):
            got = refs[:n]
            del refs[:n]
            return got

        att = take(chunks)
        stack_ref, weight_ref = take(2)
        far, near, mid = take(chunks), take(chunks), take(chunks)
        finish(chunks, seq, norm, att, stack_ref, weight_ref, far, near, mid, *refs)

    return pl.pallas_call(
        kernel,
        in_specs=[vmem] * (4 * chunks + 4),
        out_specs=[vmem] * 4,
        out_shape=[
            jax.ShapeDtypeStruct((rows, width), BF16),
            jax.ShapeDtypeStruct((rows, depth), BF16),
            jax.ShapeDtypeStruct((rows, depth), BF16),
            jax.ShapeDtypeStruct((depth, piece), F32),
        ],
        scratch_shapes=[
            pltpu.VMEM((2, RIM, part), BF16),
            pltpu.VMEM(rim, BF16),
            pltpu.VMEM(rim, BF16),
            pltpu.VMEM((4, part, piece), BF16),
            pltpu.VMEM((4, part, piece), BF16),
            pltpu.VMEM((4, depth, piece), F32),
            pltpu.VMEM((2, depth, piece), BF16),
            pltpu.VMEM((2, depth, piece), BF16),
            pltpu.VMEM((depth, piece), BF16),
            pltpu.VMEM((depth, piece), BF16),
            pltpu.VMEM((2, rows, width), BF16),
            pltpu.VMEM((2, rows, width), BF16),
            pltpu.VMEM((rows, width), F32),
            pltpu.VMEM((rows, width), F32),
            pltpu.VMEM((rows, width), BF16),
            pltpu.VMEM((rows, width), BF16),
            sem((1,)), sem((1,)), sem((chunks,)), sem((chunks,)),
            sem((4,)), sem((4,)), sem((2,)), sem((2,)), sem((1,)), sem((1,)),
            sem((2,)), sem((2,)), sem((1,)), sem((1,)),
        ],
        compiler_params=pltpu.CompilerParams(
            collective_id=0, has_side_effects=True, vmem_limit_bytes=60 << 20
        ),
        cost_estimate=pl.CostEstimate(
            flops=4 * rows * depth * width * 4, bytes_accessed=40 << 20, transcendentals=0
        ),
    )(*atts, stacked, weight, *fars, *nears, *mids, relay, crossed)


def local(queries, key_rows, value_rows, out_weight, cotangent, neighbours):
    rows, columns = queries.shape
    heads = columns // HD
    tiles = rows // TILE
    seq, head = lax.axis_size("seq"), lax.axis_size("head")
    s, h = lax.axis_index("seq"), lax.axis_index("head")
    paired = head == 4 and seq == 8
    width = cotangent.shape[1]
    piece = width * head // seq
    norm = 1.0 / math.sqrt(rows * seq)
    chunks = 2
    per = heads // chunks

    halos = []
    for n in range(chunks):
        cut = slice(n * per * HD, (n + 1) * per * HD)
        kv = jnp.stack([key_rows[:, cut], value_rows[:, cut]])
        near = swap(kv, "seq", 1)
        far = shift(near, "seq", 2)
        halos.append((far, near))

    if paired:
        shards = [cotangent, swap(cotangent, "head", 1), swap(cotangent, "head", 2)]
        shards.append(swap(shards[2], "head", 1))
        weights = [
            lax.dynamic_slice_in_dim(out_weight, (h ^ r) * width, width, 1) for r in range(4)
        ]
        grad_attention = sum(dot_nt(a, b) for a, b in zip(shards, weights)).astype(BF16)
    else:
        full = lax.all_gather(cotangent, "head", axis=1, tiled=True)
        grad_attention = dot_nt(full, out_weight).astype(BF16)

    first = s * tiles - REACH
    alive = neighbours >= 0
    index = jnp.where(alive, neighbours - first, 0)
    span = tiles + REACH
    odd = s % 2 == 1
    turned = jnp.where(index < REACH, index + span, jnp.where(index >= span, index - span, index))
    place = jnp.where(odd, turned, index).reshape(-1).astype(jnp.int32)
    count = jnp.sum(alive, axis=1).astype(jnp.int32)

    atts, dqs, mids, fars, nears = [], [], [], [], []
    if paired:
        stacked = jnp.stack(shards)
        turned = ((h ^ (s // 2)) ^ jnp.arange(4, dtype=jnp.int32)).astype(jnp.int32)
        side = (s % 2).astype(jnp.int32).reshape(1)
        place, stacked = lax.optimization_barrier((place, stacked))
    for n in range(chunks):
        far, near = halos[n]
        if n == 1 and paired:
            place, relay = lax.optimization_barrier((place, fars[0]))
            relay = shift(relay, "seq", -2)
            away = away_call(turned, side, atts[0], stacked, piece)
            place, away = lax.optimization_barrier((place, away))
            crossed = swap(away, "seq", 1)
        att, dq, mid, rim_far, rim_near = attention_call(
            place, count, queries, grad_attention, key_rows, value_rows, far, near, n * per, per
        )
        atts.append(att)
        dqs.append(dq)
        mids.append(mid)
        fars.append(rim_far)
        nears.append(rim_near)

    grad_queries = jnp.concatenate(dqs, axis=1)
    if paired:
        projected, grad_keys, grad_values, grad_weight = finish_call(
            atts, stacked, out_weight, fars, nears, mids, relay, crossed, seq, norm
        )
        return (projected, grad_queries, grad_keys, grad_values, grad_weight)

    dks, dvs = [], []
    for n in range(chunks):
        relayed = shift(fars[n], "seq", -2)
        back = swap((nears[n] + relayed.astype(F32)).astype(BF16), "seq", 1)
        done = (mids[n] + back.astype(F32)).astype(BF16)
        dks.append(done[0])
        dvs.append(done[1])
    attention = jnp.concatenate(atts, axis=1)
    projected = lax.psum_scatter(
        dot_nn(attention, out_weight).astype(BF16), "head", scatter_dimension=1, tiled=True
    )
    grad_weight = (
        lax.psum_scatter(
            dot_tn(attention, full).astype(BF16), "seq", scatter_dimension=1, tiled=True
        ).astype(F32)
        * norm
    )
    return (
        projected,
        grad_queries,
        jnp.concatenate(dks, axis=1),
        jnp.concatenate(dvs, axis=1),
        grad_weight,
    )


def solution(mesh):
    both = P("seq", "head")
    return jax.shard_map(
        local,
        mesh=mesh,
        in_specs=(both, both, both, P("head", None), both, P("seq", None)),
        out_specs=(both, both, both, both, P("head", "seq")),
        check_vma=False,
    )
```
